512 devices in a mesh: seq: 64 (over y, z_lo, x), tp: 8 (over z_hi, core).
Axes of the slice: x: 4, y: 4, z: 16 (z_hi: 4, z_lo: 4; z = z_hi * 4 + z_lo), core: 2. Of those that a mesh axis runs over, the one named last changes fastest.
Arguments:
- video_tokens: bfloat16 [8192, 5120], P('seq'), may hold values from -40 to 40
- w_query: bfloat16 [5120, 5120], P('seq', 'tp'), may hold values from -1 to 1
- text_keys: bfloat16 [128, 5120], P(None, 'tp'), may hold values from -4 to 4
- text_values: bfloat16 [128, 5120], P(None, 'tp'), may hold values from -4 to 4
- grad_out: bfloat16 [8192, 5120], P('seq', 'tp'), may hold values from -5 to 5
Outputs:
- grad_video: bfloat16 [8192, 5120], P(('seq', 'tp'))
- grad_keys: bfloat16 [128, 5120], P('seq', 'tp')
- grad_values: bfloat16 [128, 5120], P('seq', 'tp')
The draws below stay inside these ranges and needn't reach their ends.
All inputs are finite; a program needn't handle non-finite values.
Results may differ from the reference program's by a relative error of at most 0.014.
Values may be sent and summed in bfloat16 or wider, within the bound.
A program may use at most 64 MiB of HBM per device.

```python
import math
import jax
import jax.numpy as jnp
from jax import lax

D = 5120
HEADS = 40
HEAD_DIM = 128
TOKENS = 8192
TEXT = 128
N_TP = 8


def draw_together(key):
    seeded = jax.random.fold_in(key, 4099)
    key_video, key_weight, key_text = jax.random.split(seeded, 3)
    width = HEADS * HEAD_DIM
    weight = jnp.clip(jax.random.normal(key_weight, (D, width), jnp.float32), -4.0, 4.0) * D ** (-0.5)
    video = jnp.clip(jax.random.normal(key_video, (TOKENS, D), jnp.float32), -4.0, 4.0)
    keys_all = jnp.clip(jax.random.normal(key_text, (TEXT, width), jnp.float32), -4.0, 4.0)
    return (video, weight, keys_all)


def draw_video_tokens(key, part):
    return draw_together(key)[0].astype(jnp.bfloat16)


def draw_w_query(key, part):
    return draw_together(key)[1].astype(jnp.bfloat16)


def draw_text_keys(key, part):
    return draw_together(key)[2].astype(jnp.bfloat16)


def steps_of(stream_key, extent, cuts, low, high):
    factor_of = 1.0
    for axis_at, shards_of in cuts:
        heights = jax.random.uniform(jax.random.fold_in(jax.random.fold_in(stream_key, 6), axis_at), (shards_of,), jnp.float32, low / len(cuts), high / len(cuts))
        factor_of = factor_of * jnp.repeat(jnp.exp(heights), extent[axis_at] // shards_of).reshape((-1,) + (1,) * (len(extent) - 1 - axis_at))
    return factor_of


def gaussian(rng, shape, spread, most, pieces=(), dtype=jnp.bfloat16):
    drawn = jax.random.normal(rng, shape, jnp.float32) * spread
    if len(pieces) > 0:
        drawn = steps_of(rng, shape, pieces, -0.22, 0.18) * drawn
    return jnp.clip(drawn, min=-most, max=most).astype(dtype)


def setup_inputs(seed: int = 0) -> dict:
    key_list = jax.random.split(jax.random.key(seed), 6)
    video_tokens = draw_video_tokens(jax.random.fold_in(key_list[5], 71), 0)
    w_query = draw_w_query(jax.random.fold_in(key_list[5], 71), 0)
    text_keys = draw_text_keys(jax.random.fold_in(key_list[5], 71), 0)
    text_values = gaussian(key_list[3], (TEXT, HEADS * HEAD_DIM), 1.0, 4.0, ((1, 8),))
    grad_out = gaussian(key_list[4], (TOKENS, HEADS * HEAD_DIM), 1.0, 5.0, ((0, 64), (1, 8)))
    return dict(video_tokens=video_tokens, w_query=w_query, text_keys=text_keys, text_values=text_values, grad_out=grad_out)


def reference(video_tokens, w_query, text_keys, text_values, grad_out):
    factor = HEAD_DIM ** -0.5
    width = HEADS * HEAD_DIM
    query = jnp.dot(video_tokens, w_query, preferred_element_type=jnp.float32).astype(jnp.bfloat16)
    key_heads = text_keys.astype(jnp.float32).reshape(TEXT, HEADS, HEAD_DIM)
    value_heads = text_values.astype(jnp.float32).reshape(TEXT, HEADS, HEAD_DIM)
    block_len = math.gcd(TOKENS, 512)
    blocks = TOKENS // block_len
    query_blocks = query.reshape(blocks, block_len, width)
    grad_blocks = grad_out.reshape(blocks, block_len, width)

    def step_block(carry, inputs):
        key_sum, value_sum = carry
        query_rows, grad_rows = inputs
        query_heads = query_rows.astype(jnp.float32).reshape(block_len, HEADS, HEAD_DIM)
        grad_heads = grad_rows.astype(jnp.float32).reshape(block_len, HEADS, HEAD_DIM)
        scores = jnp.einsum("thd,lhd->thl", query_heads, key_heads) * factor
        row_max = jnp.max(scores, axis=2, keepdims=True)
        raised = jnp.exp(scores - row_max)
        attend = raised / jnp.sum(raised, axis=2, keepdims=True)
        attend_half = lax.optimization_barrier(attend.astype(jnp.bfloat16)).astype(jnp.float32)
        grad_attend = jnp.einsum("thd,lhd->thl", grad_heads, value_heads)
        row_dot = jnp.sum(attend * grad_attend, axis=2, keepdims=True)
        grad_scores = (attend * (grad_attend - row_dot) * factor).astype(jnp.bfloat16)
        grad_scores = lax.optimization_barrier(grad_scores).astype(jnp.float32)
        grad_query = jnp.einsum("thl,lhd->thd", grad_scores, key_heads).astype(jnp.bfloat16)
        key_sum = key_sum + jnp.einsum("thl,thd->lhd", grad_scores, query_heads)
        value_sum = value_sum + jnp.einsum("thl,thd->lhd", attend_half, grad_heads)
        return (key_sum, value_sum), grad_query.reshape(block_len, width)

    zeros_init = jnp.zeros((TEXT, HEADS, HEAD_DIM), jnp.float32)
    sums, grad_query_blocks = lax.scan(step_block, (zeros_init, zeros_init), (query_blocks, grad_blocks))
    grad_query = grad_query_blocks.reshape(TOKENS, width)
    grad_keys = sums[0].reshape(TEXT, width).astype(jnp.bfloat16)
    grad_values = sums[1].reshape(TEXT, width).astype(jnp.bfloat16)
    group_width = width // N_TP
    grad_video = jnp.zeros((TOKENS, D), jnp.float32)
    for group in range(N_TP):
        col_start = group * group_width
        col_end = col_start + group_width
        partial_sum = jnp.dot(grad_query[:, col_start:col_end], w_query[:, col_start:col_end].T, preferred_element_type=jnp.float32)
        grad_video = grad_video + lax.optimization_barrier(partial_sum.astype(jnp.bfloat16)).astype(jnp.float32)
    return grad_video.astype(jnp.bfloat16), grad_keys, grad_values
```

```python
import jax
import jax.numpy as jnp
from jax import lax
from jax.experimental import pallas as pl
from jax.experimental.pallas import tpu as pltpu
from jax.sharding import Mesh
from jax.sharding import PartitionSpec as P

HEAD_DIM = 128
HEADS = 5
ROWS = 80
TOKENS = 128
TEXT = 128
DEPTH = 5120
CHUNK = 1280
WIDTH = HEADS * HEAD_DIM
AXES = ("y", "zl", "x", "zh", "c")
SEQ = ("y", "zl", "x")
COPIES = 87
F32 = jnp.float32
BF16 = jnp.bfloat16


def dot(a, b, dims):
    return lax.dot_general(a, b, ((dims[:1], dims[1:]), ((), ())), preferred_element_type=F32)


class Mail:
    def __init__(self, send_sems, recv_sems):
        self.send_sems, self.recv_sems, self.sent = send_sems, recv_sems, []

    def send(self, src, dst, **where):
        at = len(self.sent)
        copy = pltpu.make_async_remote_copy(
            src_ref=src,
            dst_ref=dst,
            send_sem=self.send_sems.at[at],
            recv_sem=self.recv_sems.at[at],
            device_id=where,
            device_id_type=pl.DeviceIdType.MESH,
        )
        copy.start()
        self.sent.append(copy)
        return copy

    def same(self, ref, **where):
        return self.send(ref, ref, **where)


def arrived(*copies):
    for copy in copies:
        copy.wait_recv()


def kernel(
    video_hbm, weight_hbm, keys_hbm, values_hbm, grad_hbm,
    out_video, out_keys, out_values,
    video, keys_in, values_in, grad, keys, weight, grad_att, grad_query,
    kv, kv_x, kv_y, kv_mid, kv_z_src, kv_z,
    part, part_in, total, far, relay, near_up, near_down,
    local_sems, send_sems, recv_sems,
):
    y, z, x = lax.axis_index("y"), lax.axis_index("zl"), lax.axis_index("x")
    h, c = lax.axis_index("zh"), lax.axis_index("c")
    yn, yp, xn, xp = (y + 3) % 4, (y + 1) % 4, (x + 3) % 4, (x + 1) % 4
    hn, hp, hf = (h + 3) % 4, (h + 1) % 4, (h + 2) % 4
    z_others = (z + 1 - 2 * (z % 2), (z + 2) % 4, 3 - z)
    near = 2 * (z // 2)
    other = 2 - near
    factor = HEAD_DIM ** (-0.5)

    own = [
        pltpu.make_async_copy(
            weight_hbm.at[:, pl.ds(k * HEAD_DIM, HEAD_DIM)], weight.at[k, y, z, x], local_sems.at[k]
        )
        for k in range(HEADS)
    ]
    loads = [
        pltpu.make_async_copy(src, dst, local_sems.at[HEADS + k])
        for k, (src, dst) in enumerate(
            ((keys_hbm, keys_in), (values_hbm, values_in), (grad_hbm, grad), (video_hbm, video))
        )
    ]
    for copy in own + loads:
        copy.start()

    barrier = pltpu.get_barrier_semaphore()
    partners = (
        [{"zl": k} for k in z_others]
        + [{"x": k} for k in (xp, xn, (x + 2) % 4)]
        + [{"y": k} for k in (yp, yn, (y + 2) % 4)]
        + [{"zh": hp}, {"zh": hn}, {"c": 1 - c}]
    )
    for where in partners:
        pl.semaphore_signal(barrier, inc=1, device_id=where, device_id_type=pl.DeviceIdType.MESH)
    pl.semaphore_wait(barrier, len(partners))
    for copy in own:
        copy.wait()

    mail = Mail(send_sems, recv_sems)
    near_pair, other_pair = pl.ds(near, 2), pl.ds(other, 2)

    def z_step(g):
        return [mail.same(weight.at[g, y, z, x], zl=k) for k in z_others]

    def small_y(g):
        ref = weight.at[g, y, near_pair, x]
        return mail.same(ref, y=yp), mail.same(ref, y=yn)

    def small_x(g):
        ref = weight.at[g, y, other_pair, x]
        return mail.same(ref, x=xp), mail.same(ref, x=xn)

    def small_y_on(g):
        return (
            mail.same(weight.at[g, yn, near, x], y=yp),
            mail.same(weight.at[g, yp, near + 1, x], y=yn),
        )

    def small_x_on(g):
        return (
            mail.same(weight.at[g, y, other, xn], x=xp),
            mail.same(weight.at[g, y, other + 1, xp], x=xn),
        )

    def big_x(k):
        ref = weight.at[k, :, near_pair, x]
        return mail.same(ref, x=xp), mail.same(ref, x=xn)

    def big_y(k):
        ref = weight.at[k, y, other_pair]
        return mail.same(ref, y=yp), mail.same(ref, y=yn)

    def big_on(k):
        return (
            mail.same(weight.at[k, :, near, xn], x=xp),
            mail.same(weight.at[k, :, near + 1, xp], x=xn),
            mail.same(weight.at[k, yn, other], y=yp),
            mail.same(weight.at[k, yp, other + 1], y=yn),
        )

    first, rest = pl.ds(0, 1), pl.ds(1, HEADS - 1)
    z0 = z_step(first)
    z1 = z_step(rest)

    def columns(k):
        return slice(k * HEAD_DIM, (k + 1) * HEAD_DIM)

    for copy in loads[:3]:
        copy.wait()
    row = lax.broadcasted_iota(jnp.int32, (TEXT, TEXT), 0)
    col = lax.broadcasted_iota(jnp.int32, (TEXT, TEXT), 1)
    source = (row // 8 % 4) * 32 + (row // 2 % 4) * 8 + (row // 32) * 2 + row % 2
    pick = jnp.where(col == source, 1.0, 0.0).astype(BF16)
    keys[...] = dot(pick, keys_in[...], (1, 0)).astype(BF16)
    for k in range(HEADS):
        values_k = dot(pick, values_in[:, columns(k)], (1, 0)).astype(BF16)
        grad_att[k] = dot(values_k, grad[:, columns(k)], (1, 1))
    loads[3].wait()

    def attention(k):
        query = jnp.zeros((TOKENS, HEAD_DIM), F32)
        for j in range(4):
            query += dot(
                video[:, j * CHUNK : (j + 1) * CHUNK], weight[k, j].reshape(CHUNK, HEAD_DIM), (1, 0)
            )
        query = query.astype(BF16)
        keys_k = keys[:, columns(k)]
        scores = dot(keys_k, query, (1, 1)) * factor
        raised = jnp.exp(scores - jnp.max(scores, axis=0, keepdims=True))
        attend = raised / jnp.sum(raised, axis=0, keepdims=True)
        grad_attend = grad_att[k]
        row_dot = jnp.sum(attend * grad_attend, axis=0, keepdims=True)
        grad_scores = (attend * (grad_attend - row_dot) * factor).astype(BF16)
        grad_query[:, columns(k)] = dot(grad_scores, keys_k, (0, 0)).astype(BF16)
        key_part = dot(grad_scores, query, (1, 0))
        value_part = dot(attend.astype(BF16), grad[:, columns(k)], (1, 0))
        kv[0, :, :, columns(k)] = key_part.reshape(4, 32, HEAD_DIM)
        kv[1, :, :, columns(k)] = value_part.reshape(4, 32, HEAD_DIM)

    arrived(z0[0])
    y0 = small_y(first)
    arrived(*z0[1:])
    x0 = small_x(first)
    arrived(*y0)
    y0_on = small_y_on(first)
    arrived(*x0)
    x0_on = small_x_on(first)
    arrived(z1[0])
    y1 = small_y(rest)
    arrived(*z1[1:])
    x1 = small_x(rest)
    arrived(*y0_on)
    big = {}
    big[0] = big_x(0)
    arrived(*x0_on)
    big[0] += big_y(0)
    arrived(*y1)
    y1_on = small_y_on(rest)
    arrived(*x1)
    x1_on = small_x_on(rest)
    arrived(*y1_on)
    big[1] = big_x(1)
    arrived(*x1_on)
    big[1] += big_y(1)
    big_done = {}
    for k in range(HEADS):
        arrived(*big[k])
        big_done[k] = big_on(k)
        if k + 2 < HEADS:
            big[k + 2] = big_x(k + 2) + big_y(k + 2)
        if k >= 1:
            arrived(*big_done[k - 1])
            attention(k - 1)
    arrived(*big_done[HEADS - 1])
    attention(HEADS - 1)

    x_far, y_far = (x + 2) % 4, (y + 2) % 4
    kv_x_in = [
        mail.send(kv.at[:, to], kv_x.at[n], x=to) for n, to in enumerate((xp, xn, x_far))
    ]

    order = (0, 2, 1, 3)
    pair_in = {}
    for j in order:
        made = jnp.zeros((TOKENS, CHUNK), F32)
        for k in range(HEADS):
            made += dot(grad_query[:, columns(k)], weight[k, j].reshape(CHUNK, HEAD_DIM), (1, 1))
        made = made.astype(BF16)
        for t in range(8):
            part[j, t % 2, t // 2] = made[t * 16 : (t + 1) * 16]
        pair_in[j] = mail.send(part.at[j, 1 - c], part_in.at[j], c=1 - c)
    far_in, up_in, down_in = {}, {}, {}
    for j in order:
        arrived(pair_in[j])
        total[j] = (part[j, c].astype(F32) + part_in[j].astype(F32)).astype(BF16)
        if j < 2:
            far_in[j] = mail.send(total.at[j, hf], far.at[j], zh=hp)
            down_in[j] = mail.send(total.at[j, hn], near_down.at[j], zh=hn)
        else:
            far_in[j] = mail.send(total.at[j, hf], far.at[j], zh=hn)
            up_in[j] = mail.send(total.at[j, hp], near_up.at[j], zh=hp)
    for j in order:
        arrived(far_in[j])
        to = hp if j < 2 else hn
        relay[j] = (total[j, to].astype(F32) + far[j].astype(F32)).astype(BF16)
        if j < 2:
            up_in[j] = mail.send(relay.at[j], near_up.at[j], zh=hp)
        else:
            down_in[j] = mail.send(relay.at[j], near_down.at[j], zh=hn)

    arrived(*kv_x_in)
    kv_mid[...] = (kv[:, x] + kv_x[0] + kv_x[1] + kv_x[2]).reshape(2, 4, 8, WIDTH)
    kv_y_in = [
        mail.send(kv_mid.at[:, to], kv_y.at[n], y=to) for n, to in enumerate((yp, yn, y_far))
    ]
    arrived(*kv_y_in)
    mine = kv_mid[:, y] + kv_y[0] + kv_y[1] + kv_y[2]
    for j in range(4):
        kv_z_src[j] = mine[:, 2 * j : 2 * j + 2]
    kv_z_in = [
        mail.send(kv_z_src.at[to], kv_z.at[n], zl=to) for n, to in enumerate(z_others)
    ]

    for j in order:
        arrived(up_in[j], down_in[j])
        out_video[:, j * CHUNK : (j + 1) * CHUNK] = (
            total[j, h].astype(F32) + near_up[j].astype(F32) + near_down[j].astype(F32)
        ).astype(BF16)
    arrived(*kv_z_in)
    both = kv_z_src[z] + kv_z[0] + kv_z[1] + kv_z[2]
    out_keys[...] = both[0].astype(BF16)
    out_values[...] = both[1].astype(BF16)
    assert len(mail.sent) == COPIES, len(mail.sent)
    for copy in mail.sent:
        copy.wait_send()


def local(video_tokens, w_query, text_keys, text_values, grad_out):
    vmem = pltpu.VMEM
    return pl.pallas_call(
        kernel,
        out_shape=(
            jax.ShapeDtypeStruct((16, DEPTH), BF16),
            jax.ShapeDtypeStruct((2, WIDTH), BF16),
            jax.ShapeDtypeStruct((2, WIDTH), BF16),
        ),
        in_specs=[pl.BlockSpec(memory_space=pl.ANY)] * 5,
        out_specs=(pl.BlockSpec(memory_space=pltpu.VMEM),) * 3,
        scratch_shapes=[
            vmem((TOKENS, DEPTH), BF16),
            vmem((TEXT, WIDTH), BF16),
            vmem((TEXT, WIDTH), BF16),
            vmem((TOKENS, WIDTH), BF16),
            vmem((TEXT, WIDTH), BF16),
            vmem((HEADS, 4, 4, 4, ROWS, HEAD_DIM), BF16),
            vmem((HEADS, TEXT, TOKENS), F32),
            vmem((TOKENS, WIDTH), BF16),
            vmem((2, 4, 32, WIDTH), F32),
            vmem((3, 2, 32, WIDTH), F32),
            vmem((3, 2, 8, WIDTH), F32),
            vmem((2, 4, 8, WIDTH), F32),
            vmem((4, 2, 2, WIDTH), F32),
            vmem((3, 2, 2, WIDTH), F32),
            vmem((4, 2, 4, 16, CHUNK), BF16),
            vmem((4, 4, 16, CHUNK), BF16),
            vmem((4, 4, 16, CHUNK), BF16),
            vmem((4, 16, CHUNK), BF16),
            vmem((4, 16, CHUNK), BF16),
            vmem((4, 16, CHUNK), BF16),
            vmem((4, 16, CHUNK), BF16),
            pltpu.SemaphoreType.DMA((HEADS + 4,)),
            pltpu.SemaphoreType.DMA((COPIES,)),
            pltpu.SemaphoreType.DMA((COPIES,)),
        ],
        compiler_params=pltpu.CompilerParams(collective_id=0, has_side_effects=True),
    )(video_tokens, w_query, text_keys, text_values, grad_out)


def solution(mesh):
    split = Mesh(mesh.devices.reshape(4, 4, 4, 4, 2), AXES)
    tp = ("zh", "c")
    in_specs = (P(SEQ, None), P(SEQ, tp), P(None, tp), P(None, tp), P(SEQ, tp))
    out_specs = (P(AXES, None), P(SEQ, tp), P(SEQ, tp))
    return jax.shard_map(local, mesh=split, in_specs=in_specs, out_specs=out_specs, check_vma=False)
```

```python
import jax
import jax.numpy as jnp
from jax import lax
from jax.experimental import pallas as pl
from jax.experimental.pallas import tpu as pltpu
from jax.sharding import Mesh
from jax.sharding import PartitionSpec as P

HEAD_DIM = 128
HEADS = 5
ROWS = 80
TOKENS = 128
TEXT = 128
DEPTH = 5120
CHUNK = 1280
WIDTH = HEADS * HEAD_DIM
AXES = ("y", "zl", "x", "zh", "c")
SEQ = ("y", "zl", "x")
COPIES = 126
F32 = jnp.float32
BF16 = jnp.bfloat16


def dot(a, b, dims):
    return lax.dot_general(a, b, ((dims[:1], dims[1:]), ((), ())), preferred_element_type=F32)


class Mail:
    def __init__(self, send_sems, recv_sems):
        self.send_sems, self.recv_sems = send_sems, recv_sems
        self.made, self.sent = [], []

    def make(self, src, dst, **where):
        at = len(self.made)
        copy = pltpu.make_async_remote_copy(
            src_ref=src,
            dst_ref=dst,
            send_sem=self.send_sems.at[at],
            recv_sem=self.recv_sems.at[at],
            device_id=where,
            device_id_type=pl.DeviceIdType.MESH,
        )
        self.made.append(copy)
        return copy

    def send(self, src, dst, **where):
        copy = self.make(src, dst, **where)
        copy.start()
        self.sent.append(copy)
        return copy

    def same(self, ref, **where):
        return self.send(ref, ref, **where)


def arrived(*copies):
    for copy in copies:
        copy.wait_recv()


def kernel(
    video_hbm, weight_hbm, keys_hbm, values_hbm, grad_hbm,
    out_video, out_keys, out_values,
    video, keys_in, values_in, grad, keys, weight, grad_att, grad_query, made,
    kv, kv_1, kv_2, kv_mid, kv_z_src, kv_z,
    part, part_in, total, far, relay, near_up, near_down,
    local_sems, send_sems, recv_sems,
):
    y, z, x = lax.axis_index("y"), lax.axis_index("zl"), lax.axis_index("x")
    h, c = lax.axis_index("zh"), lax.axis_index("c")
    yf, xf = (y + 2) % 4, (x + 2) % 4
    yn, yp, xn, xp = (y + 3) % 4, (y + 1) % 4, (x + 3) % 4, (x + 1) % 4
    hn, hp, hf = (h + 3) % 4, (h + 1) % 4, (h + 2) % 4
    z_others = (z + 1 - 2 * (z % 2), (z + 2) % 4, 3 - z)
    near = 2 * (z // 2)
    other = 2 - near
    factor = HEAD_DIM ** (-0.5)

    own = [
        pltpu.make_async_copy(
            weight_hbm.at[:, pl.ds(k * HEAD_DIM, HEAD_DIM)], weight.at[k, y, z, x], local_sems.at[k]
        )
        for k in range(HEADS)
    ]
    loads = [
        pltpu.make_async_copy(src, dst, local_sems.at[HEADS + k])
        for k, (src, dst) in enumerate(
            ((keys_hbm, keys_in), (values_hbm, values_in), (grad_hbm, grad), (video_hbm, video))
        )
    ]
    for copy in own + loads:
        copy.start()

    barrier = pltpu.get_barrier_semaphore()
    partners = (
        [{"zl": k} for k in z_others]
        + [{"x": k} for k in (xp, xn, (x + 2) % 4)]
        + [{"y": k} for k in (yp, yn, (y + 2) % 4)]
        + [{"zh": hp}, {"zh": hn}, {"c": 1 - c}]
    )
    for where in partners:
        pl.semaphore_signal(barrier, inc=1, device_id=where, device_id_type=pl.DeviceIdType.MESH)
    pl.semaphore_wait(barrier, len(partners))
    for copy in own:
        copy.wait()

    mail = Mail(send_sems, recv_sems)
    near_pair, other_pair = pl.ds(near, 2), pl.ds(other, 2)

    def z_step(g):
        return [mail.same(weight.at[g, y, z, x], zl=k) for k in z_others]

    def small_y(g):
        ref = weight.at[g, y, near_pair, x]
        return mail.same(ref, y=yp), mail.same(ref, y=yn)

    def small_x(g):
        ref = weight.at[g, y, other_pair, x]
        return mail.same(ref, x=xp), mail.same(ref, x=xn)

    def small_y_on(g):
        return (
            mail.same(weight.at[g, yn, near, x], y=yp),
            mail.same(weight.at[g, yp, near + 1, x], y=yn),
        )

    def small_x_on(g):
        return (
            mail.same(weight.at[g, y, other, xn], x=xp),
            mail.same(weight.at[g, y, other + 1, xp], x=xn),
        )

    def big_x(k):
        ref = weight.at[k, :, near_pair, x]
        return mail.same(ref, x=xp), mail.same(ref, x=xn)

    def big_y(k):
        ref = weight.at[k, y, other_pair]
        return mail.same(ref, y=yp), mail.same(ref, y=yn)

    def big_on(k):
        return (
            mail.same(weight.at[k, :, near, xn], x=xp),
            mail.same(weight.at[k, :, near + 1, xp], x=xn),
            mail.same(weight.at[k, yn, other], y=yp),
            mail.same(weight.at[k, yp, other + 1], y=yn),
        )

    last = HEADS - 1
    rows_a, rows_b = pl.ds(0, 40), pl.ds(40, 40)
    single, double = (lambda k: pl.ds(k, 1)), pl.ds(2, 2)
    z0 = z_step(single(0))
    a_ref, b_ref = weight.at[last, y, z, x, rows_a], weight.at[last, y, z, x, rows_b]
    a1 = [mail.same(a_ref, x=to) for to in (xp, xn, (x + 2) % 4)]
    b1 = [mail.same(b_ref, y=to) for to in (yp, yn, (y + 2) % 4)]
    z1 = z_step(single(1))
    z2 = z_step(double)

    def by_x(ref):
        return mail.same(ref, x=xp), mail.same(ref, x=xn)

    def by_y(ref):
        return mail.same(ref, y=yp), mail.same(ref, y=yn)

    def columns(k):
        return slice(k * HEAD_DIM, (k + 1) * HEAD_DIM)

    for copy in loads[:3]:
        copy.wait()
    row = lax.broadcasted_iota(jnp.int32, (TEXT, TEXT), 0)
    col = lax.broadcasted_iota(jnp.int32, (TEXT, TEXT), 1)
    source = (row // 8 % 4) * 32 + (row // 2 % 4) * 8 + (row // 32) * 2 + row % 2
    pick = jnp.where(col == source, 1.0, 0.0).astype(BF16)
    keys[...] = dot(pick, keys_in[...], (1, 0)).astype(BF16)
    loads[3].wait()

    def prepare():
        for k in range(HEADS):
            values_k = dot(pick, values_in[:, columns(k)], (1, 0)).astype(BF16)
            grad_att[k] = dot(values_k, grad[:, columns(k)], (1, 1))

    def attention(k):
        query = jnp.zeros((TOKENS, HEAD_DIM), F32)
        for j in range(4):
            query += dot(
                video[:, j * CHUNK : (j + 1) * CHUNK], weight[k, j].reshape(CHUNK, HEAD_DIM), (1, 0)
            )
        query = query.astype(BF16)
        keys_k = keys[:, columns(k)]
        scores = dot(keys_k, query, (1, 1)) * factor
        raised = jnp.exp(scores - jnp.max(scores, axis=0, keepdims=True))
        attend = raised / jnp.sum(raised, axis=0, keepdims=True)
        grad_attend = grad_att[k]
        row_dot = jnp.sum(attend * grad_attend, axis=0, keepdims=True)
        grad_scores = (attend * (grad_attend - row_dot) * factor).astype(BF16)
        grad_query[:, columns(k)] = dot(grad_scores, keys_k, (0, 0)).astype(BF16)
        key_part = dot(grad_scores, query, (1, 0))
        value_part = dot(attend.astype(BF16), grad[:, columns(k)], (1, 0))
        kv[0, :, :, :, columns(k)] = key_part.reshape(4, 4, 8, HEAD_DIM)
        kv[1, :, :, :, columns(k)] = value_part.reshape(4, 4, 8, HEAD_DIM)

    def back(k, j):
        return dot(grad_query[:, columns(k)], weight[k, j].reshape(CHUNK, HEAD_DIM), (1, 1))

    def gather_back(k):
        for j in range(4):
            made[j] = back(k, j) if k == 0 else made[j] + back(k, j)

    def small_a():
        ref = weight.at[last, y, z, :, rows_a]
        return mail.same(ref, y=yp), mail.same(ref, y=yn)

    def small_b():
        ref = weight.at[last, :, z, x, rows_b]
        return mail.same(ref, x=xp), mail.same(ref, x=xn)

    sent_if = []

    def plane_send(which, go, to):
        ref = weight.at[last, :, which]
        copy = mail.make(ref, ref, zl=to)
        pl.when(go)(copy.start)
        sent_if.append((copy, go))
        return copy

    def plane_arrived(copy, go):
        pl.when(go)(copy.wait_recv)

    z_up, z_down = (z + 1) % 4, (z + 3) % 4

    def planes(step):
        lower, upper = (z + 4 - step) % 4, (z + step) % 4
        up = plane_send(lower, jnp.logical_and(z >= step, z < 3), z_up)
        down = plane_send(upper, jnp.logical_and(z + step <= 3, z > 0), z_down)
        return up, down

    def planes_in(copies, step):
        plane_arrived(copies[0], z >= step + 1)
        plane_arrived(copies[1], z + step + 1 <= 3)

    prepare()
    arrived(z0[0])
    y0 = small_y(single(0))
    slices = by_x(weight.at[0, y, near_pair, x])
    arrived(*z0[1:])
    x0 = small_x(single(0))
    slices += by_y(weight.at[0, y, other_pair, x])
    arrived(*a1)
    a2 = small_a()
    arrived(*b1)
    b2 = small_b()
    arrived(*y0)
    y0_on = small_y_on(single(0))
    slices += by_x(weight.at[0, yn, near_pair, x]) + by_x(weight.at[0, yp, near_pair, x])
    arrived(z1[0])
    y1 = small_y(single(1))
    arrived(*x0)
    x0_on = small_x_on(single(0))
    slices += by_y(weight.at[0, y, other_pair, xn]) + by_y(weight.at[0, y, other_pair, xp])
    arrived(*z1[1:])
    x1 = small_x(single(1))
    arrived(*y0_on)
    slices += by_x(weight.at[0, yf, near_pair, x])
    arrived(*a2)
    a2_on = mail.same(weight.at[last, yn, z, :, rows_a], y=yp)
    arrived(*b2)
    b2_on = mail.same(weight.at[last, :, z, xn, rows_b], x=xp)
    arrived(*x0_on)
    slices += by_y(weight.at[0, y, other_pair, xf])
    big, big_done, plane = {}, {}, {}
    arrived(*y1)
    y1_on = small_y_on(single(1))
    arrived(*x1)
    x1_on = small_x_on(single(1))
    arrived(z2[0])
    y2 = small_y(double)
    arrived(*z2[1:])
    x2 = small_x(double)
    arrived(a2_on, b2_on)
    plane[0] = planes(0)
    arrived(*y1_on)
    big[1] = big_x(1)
    arrived(*x1_on)
    big[1] += big_y(1)
    arrived(*y2)
    y2_on = small_y_on(double)
    arrived(*x2)
    x2_on = small_x_on(double)
    arrived(*slices)
    big_done[0] = big_on(0)
    arrived(*y2_on, *x2_on)
    big[2] = big_x(2) + big_y(2)
    arrived(*big[1])
    big_done[1] = big_on(1)
    big[3] = big_x(3) + big_y(3)
    planes_in(plane[0], 0)
    plane[1] = planes(1)
    arrived(*big_done[0])
    attention(0)
    gather_back(0)
    arrived(*big[2])
    big_done[2] = big_on(2)
    arrived(*big_done[1])
    attention(1)
    gather_back(1)
    planes_in(plane[1], 1)
    plane[2] = planes(2)
    arrived(*big[3])
    big_done[3] = big_on(3)
    arrived(*big_done[2])
    attention(2)
    gather_back(2)
    arrived(*big_done[3])
    planes_in(plane[2], 2)
    attention(3)
    attention(4)

    key_in = [mail.send(kv.at[0, to], kv_1.at[0, n], x=to) for n, to in enumerate((xp, xn, xf))]
    value_in = [mail.send(kv.at[1, :, to], kv_1.at[1, n], y=to) for n, to in enumerate((yp, yn, yf))]

    order = (0, 2, 1, 3)
    pair_in, far_in, up_in, down_in = {}, {}, {}, {}

    def make_part(j):
        whole = (made[j] + back(3, j) + back(4, j)).astype(BF16)
        for t in range(8):
            part[j, t % 2, t // 2] = whole[t * 16 : (t + 1) * 16]
        pair_in[j] = mail.send(part.at[j, 1 - c], part_in.at[j], c=1 - c)

    def make_total(j):
        arrived(pair_in[j])
        total[j] = (part[j, c].astype(F32) + part_in[j].astype(F32)).astype(BF16)
        to = hp if j < 2 else hn
        far_in[j] = mail.send(total.at[j, hf], far.at[j], zh=to)

    def send_on(j):
        arrived(far_in[j])
        to = hp if j < 2 else hn
        relay[j] = (total[j, to].astype(F32) + far[j].astype(F32)).astype(BF16)
        if j < 2:
            up_in[j] = mail.send(relay.at[j], near_up.at[j], zh=hp)
        else:
            down_in[j] = mail.send(relay.at[j], near_down.at[j], zh=hn)

    make_part(0)
    make_part(2)
    make_part(1)
    make_total(0)
    make_part(3)
    make_total(2)
    make_total(1)
    make_total(3)
    for j in (0, 1):
        down_in[j] = mail.send(total.at[j, hn], near_down.at[j], zh=hn)
        up_in[j + 2] = mail.send(total.at[j + 2, hp], near_up.at[j + 2], zh=hp)

    arrived(*key_in)
    kv_mid[0] = kv[0, x] + kv_1[0, 0] + kv_1[0, 1] + kv_1[0, 2]
    key_in = [mail.send(kv_mid.at[0, to], kv_2.at[0, n], y=to) for n, to in enumerate((yp, yn, yf))]
    arrived(*value_in)
    kv_mid[1] = kv[1, :, y] + kv_1[1, 0] + kv_1[1, 1] + kv_1[1, 2]
    value_in = [mail.send(kv_mid.at[1, to], kv_2.at[1, n], x=to) for n, to in enumerate((xp, xn, xf))]
    send_on(0)
    send_on(2)
    arrived(*key_in, *value_in)
    for k, at in enumerate((y, x)):
        rows = kv_mid[k, at] + kv_2[k, 0] + kv_2[k, 1] + kv_2[k, 2]
        for j in range(4):
            kv_z_src[j, k] = rows[2 * j : 2 * j + 2]
    kv_z_in = [mail.send(kv_z_src.at[to], kv_z.at[n], zl=to) for n, to in enumerate(z_others)]
    send_on(1)
    send_on(3)

    for j in order:
        arrived(up_in[j], down_in[j])
        out_video[:, j * CHUNK : (j + 1) * CHUNK] = (
            total[j, h].astype(F32) + near_up[j].astype(F32) + near_down[j].astype(F32)
        ).astype(BF16)
    arrived(*kv_z_in)
    both = kv_z_src[z] + kv_z[0] + kv_z[1] + kv_z[2]
    out_keys[...] = both[0].astype(BF16)
    out_values[...] = both[1].astype(BF16)
    assert len(mail.made) == COPIES, len(mail.made)
    for copy in mail.sent:
        copy.wait_send()
    for copy, go in sent_if:
        pl.when(go)(copy.wait_send)


def hand_over(a_in, b_in, c_in, a_out, b_out, c_out):
    a_out[...] = a_in[...]
    b_out[...] = b_in[...]
    c_out[...] = c_in[...]


def local(video_tokens, w_query, text_keys, text_values, grad_out):
    vmem = pltpu.VMEM
    out_shape = (
        jax.ShapeDtypeStruct((16, DEPTH), BF16),
        jax.ShapeDtypeStruct((2, WIDTH), BF16),
        jax.ShapeDtypeStruct((2, WIDTH), BF16),
    )
    results = pl.pallas_call(
        kernel,
        out_shape=out_shape,
        in_specs=[pl.BlockSpec(memory_space=pl.ANY)] * 5,
        out_specs=(pl.BlockSpec(memory_space=pltpu.VMEM),) * 3,
        scratch_shapes=[
            vmem((TOKENS, DEPTH), BF16),
            vmem((TEXT, WIDTH), BF16),
            vmem((TEXT, WIDTH), BF16),
            vmem((TOKENS, WIDTH), BF16),
            vmem((TEXT, WIDTH), BF16),
            vmem((HEADS, 4, 4, 4, ROWS, HEAD_DIM), BF16),
            vmem((HEADS, TEXT, TOKENS), F32),
            vmem((TOKENS, WIDTH), BF16),
            vmem((4, TOKENS, CHUNK), F32),
            vmem((2, 4, 4, 8, WIDTH), F32),
            vmem((2, 3, 4, 8, WIDTH), F32),
            vmem((2, 3, 8, WIDTH), F32),
            vmem((2, 4, 8, WIDTH), F32),
            vmem((4, 2, 2, WIDTH), F32),
            vmem((3, 2, 2, WIDTH), F32),
            vmem((4, 2, 4, 16, CHUNK), BF16),
            vmem((4, 4, 16, CHUNK), BF16),
            vmem((4, 4, 16, CHUNK), BF16),
            vmem((4, 16, CHUNK), BF16),
            vmem((4, 16, CHUNK), BF16),
            vmem((4, 16, CHUNK), BF16),
            vmem((4, 16, CHUNK), BF16),
            pltpu.SemaphoreType.DMA((HEADS + 4,)),
            pltpu.SemaphoreType.DMA((COPIES,)),
            pltpu.SemaphoreType.DMA((COPIES,)),
        ],
        compiler_params=pltpu.CompilerParams(collective_id=0, has_side_effects=True),
    )(video_tokens, w_query, text_keys, text_values, grad_out)
    return pl.pallas_call(
        hand_over,
        out_shape=out_shape,
        in_specs=[pl.BlockSpec(memory_space=pltpu.VMEM)] * 3,
        out_specs=(pl.BlockSpec(memory_space=pltpu.VMEM),) * 3,
    )(*results)


def solution(mesh):
    split = Mesh(mesh.devices.reshape(4, 4, 4, 4, 2), AXES)
    tp = ("zh", "c")
    in_specs = (P(SEQ, None), P(SEQ, tp), P(None, tp), P(None, tp), P(SEQ, tp))
    out_specs = (P(AXES, None), P(SEQ, tp), P(SEQ, tp))
    return jax.shard_map(local, mesh=split, in_specs=in_specs, out_specs=out_specs, check_vma=False)
```

```python
import jax
import jax.numpy as jnp
from jax import lax
from jax.experimental import pallas as pl
from jax.experimental.pallas import tpu as pltpu
from jax.sharding import Mesh
from jax.sharding import PartitionSpec as P

HEAD_DIM = 128
HEADS = 5
ROWS = 80
TOKENS = 128
TEXT = 128
DEPTH = 5120
CHUNK = 1280
WIDTH = HEADS * HEAD_DIM
AXES = ("y", "zl", "x", "zh", "c")
SEQ = ("y", "zl", "x")
COPIES = 132
F32 = jnp.float32
BF16 = jnp.bfloat16


def dot(a, b, dims):
    return lax.dot_general(a, b, ((dims[:1], dims[1:]), ((), ())), preferred_element_type=F32)


class Mail:
    def __init__(self, send_sems, recv_sems):
        self.send_sems, self.recv_sems = send_sems, recv_sems
        self.made, self.sent = [], []

    def make(self, src, dst, **where):
        at = len(self.made)
        copy = pltpu.make_async_remote_copy(
            src_ref=src,
            dst_ref=dst,
            send_sem=self.send_sems.at[at],
            recv_sem=self.recv_sems.at[at],
            device_id=where,
            device_id_type=pl.DeviceIdType.MESH,
        )
        self.made.append(copy)
        return copy

    def send(self, src, dst, **where):
        copy = self.make(src, dst, **where)
        copy.start()
        self.sent.append(copy)
        return copy

    def same(self, ref, **where):
        return self.send(ref, ref, **where)


def arrived(*copies):
    for copy in copies:
        copy.wait_recv()


def kernel(
    video_hbm, weight_hbm, keys_hbm, values_hbm, grad_hbm,
    out_video, out_keys, out_values,
    video, keys_in, values_in, grad, keys, weight, grad_att, grad_query, made,
    kv, kv_1, kv_2, kv_mid, kv_z_src, kv_z,
    part, part_in, total, far, relay, near_up, near_down,
    local_sems, send_sems, recv_sems,
):
    y, z, x = lax.axis_index("y"), lax.axis_index("zl"), lax.axis_index("x")
    h, c = lax.axis_index("zh"), lax.axis_index("c")
    yf, xf = (y + 2) % 4, (x + 2) % 4
    yn, yp, xn, xp = (y + 3) % 4, (y + 1) % 4, (x + 3) % 4, (x + 1) % 4
    hn, hp, hf = (h + 3) % 4, (h + 1) % 4, (h + 2) % 4
    z_others = (z + 1 - 2 * (z % 2), (z + 2) % 4, 3 - z)
    near = 2 * (z // 2)
    other = 2 - near
    factor = HEAD_DIM ** (-0.5)

    own = [
        pltpu.make_async_copy(
            weight_hbm.at[:, pl.ds(k * HEAD_DIM, HEAD_DIM)], weight.at[k, y, z, x], local_sems.at[k]
        )
        for k in range(HEADS)
    ]
    loads = [
        pltpu.make_async_copy(src, dst, local_sems.at[HEADS + k])
        for k, (src, dst) in enumerate(
            ((keys_hbm, keys_in), (values_hbm, values_in), (grad_hbm, grad), (video_hbm, video))
        )
    ]
    for copy in own + loads:
        copy.start()

    barrier = pltpu.get_barrier_semaphore()
    partners = (
        [{"zl": k} for k in z_others]
        + [{"x": k} for k in (xp, xn, (x + 2) % 4)]
        + [{"y": k} for k in (yp, yn, (y + 2) % 4)]
        + [{"zh": hp}, {"zh": hn}, {"c": 1 - c}]
    )
    for where in partners:
        pl.semaphore_signal(barrier, inc=1, device_id=where, device_id_type=pl.DeviceIdType.MESH)
    pl.semaphore_wait(barrier, len(partners))
    for copy in own:
        copy.wait()

    mail = Mail(send_sems, recv_sems)
    near_pair, other_pair = pl.ds(near, 2), pl.ds(other, 2)

    def z_step(g):
        return [mail.same(weight.at[g, y, z, x], zl=k) for k in z_others]

    def small_y(g):
        ref = weight.at[g, y, near_pair, x]
        return mail.same(ref, y=yp), mail.same(ref, y=yn)

    def small_x(g):
        ref = weight.at[g, y, other_pair, x]
        return mail.same(ref, x=xp), mail.same(ref, x=xn)

    def small_y_on(g):
        return (
            mail.same(weight.at[g, yn, near, x], y=yp),
            mail.same(weight.at[g, yp, near + 1, x], y=yn),
        )

    def small_x_on(g):
        return (
            mail.same(weight.at[g, y, other, xn], x=xp),
            mail.same(weight.at[g, y, other + 1, xp], x=xn),
        )

    def big_x(k):
        ref = weight.at[k, :, near_pair, x]
        return mail.same(ref, x=xp), mail.same(ref, x=xn)

    def big_y(k):
        ref = weight.at[k, y, other_pair]
        return mail.same(ref, y=yp), mail.same(ref, y=yn)

    def big_on(k):
        return (
            mail.same(weight.at[k, :, near, xn], x=xp),
            mail.same(weight.at[k, :, near + 1, xp], x=xn),
            mail.same(weight.at[k, yn, other], y=yp),
            mail.same(weight.at[k, yp, other + 1], y=yn),
        )

    last = HEADS - 1
    rows_a, rows_b = pl.ds(0, 40), pl.ds(40, 40)
    single, double = (lambda k: pl.ds(k, 1)), pl.ds(2, 2)
    z0 = z_step(single(0))
    a_ref, b_ref = weight.at[last, y, z, x, rows_a], weight.at[last, y, z, x, rows_b]
    a1 = [mail.same(a_ref, x=to) for to in (xp, xn, (x + 2) % 4)]
    b1 = [mail.same(b_ref, y=to) for to in (yp, yn, (y + 2) % 4)]
    z1 = z_step(single(1))
    z2 = z_step(double)

    def by_x(ref):
        return mail.same(ref, x=xp), mail.same(ref, x=xn)

    def by_y(ref):
        return mail.same(ref, y=yp), mail.same(ref, y=yn)

    def columns(k):
        return slice(k * HEAD_DIM, (k + 1) * HEAD_DIM)

    for copy in loads[:3]:
        copy.wait()
    row = lax.broadcasted_iota(jnp.int32, (TEXT, TEXT), 0)
    col = lax.broadcasted_iota(jnp.int32, (TEXT, TEXT), 1)
    source = (row // 8 % 4) * 32 + (row // 2 % 4) * 8 + (row // 32) * 2 + row % 2
    pick = jnp.where(col == source, 1.0, 0.0).astype(BF16)
    keys[...] = dot(pick, keys_in[...], (1, 0)).astype(BF16)
    loads[3].wait()

    def prepare():
        for k in range(HEADS):
            values_k = dot(pick, values_in[:, columns(k)], (1, 0)).astype(BF16)
            grad_att[k] = dot(values_k, grad[:, columns(k)], (1, 1))

    def attention(k):
        parts = [
            dot(video[:, j * CHUNK : (j + 1) * CHUNK], weight[k, j].reshape(CHUNK, HEAD_DIM), (1, 0))
            for j in range(4)
        ]
        query = (parts[0] + parts[1] + (parts[2] + parts[3])).astype(BF16)
        keys_k = keys[:, columns(k)]
        scores = dot(keys_k, query, (1, 1)) * factor
        raised = jnp.exp(scores - jnp.max(scores, axis=0, keepdims=True))
        attend = raised / jnp.sum(raised, axis=0, keepdims=True)
        grad_attend = grad_att[k]
        row_dot = jnp.sum(attend * grad_attend, axis=0, keepdims=True)
        grad_scores = (attend * (grad_attend - row_dot) * factor).astype(BF16)
        grad_query[:, columns(k)] = dot(grad_scores, keys_k, (0, 0)).astype(BF16)
        key_part = dot(grad_scores, query, (1, 0))
        value_part = dot(attend.astype(BF16), grad[:, columns(k)], (1, 0))
        kv[0, :, :, :, columns(k)] = key_part.reshape(4, 4, 8, HEAD_DIM)
        kv[1, :, :, :, columns(k)] = value_part.reshape(4, 4, 8, HEAD_DIM)

    def back(k, j):
        return dot(grad_query[:, columns(k)], weight[k, j].reshape(CHUNK, HEAD_DIM), (1, 1))

    def gather_back(k):
        for j in range(4):
            made[j] = back(k, j) if k == 0 else made[j] + back(k, j)

    def small_a():
        ref = weight.at[last, y, z, :, rows_a]
        return mail.same(ref, y=yp), mail.same(ref, y=yn)

    def small_b():
        ref = weight.at[last, :, z, x, rows_b]
        return mail.same(ref, x=xp), mail.same(ref, x=xn)

    sent_if = []

    def plane_send(which, half, go, to):
        ref = weight.at[last, pl.ds(2 * half, 2), which]
        copy = mail.make(ref, ref, zl=to)
        pl.when(go)(copy.start)
        sent_if.append((copy, go))
        return copy

    def plane_arrived(copy, go):
        pl.when(go)(copy.wait_recv)

    z_up, z_down = (z + 1) % 4, (z + 3) % 4

    def planes(step, half):
        lower, upper = (z + 4 - step) % 4, (z + step) % 4
        up = plane_send(lower, half, jnp.logical_and(z >= step, z < 3), z_up)
        down = plane_send(upper, half, jnp.logical_and(z + step <= 3, z > 0), z_down)
        return up, down

    def planes_in(copies, step):
        plane_arrived(copies[0], z >= step + 1)
        plane_arrived(copies[1], z + step + 1 <= 3)

    prepare()
    arrived(*a1)
    a2 = small_a()
    arrived(*b1)
    b2 = small_b()
    arrived(z0[0])
    y0 = small_y(single(0))
    slices = by_x(weight.at[0, y, near_pair, x])
    arrived(*z0[1:])
    x0 = small_x(single(0))
    slices += by_y(weight.at[0, y, other_pair, x])
    arrived(*y0)
    y0_on = small_y_on(single(0))
    slices += by_x(weight.at[0, yn, near_pair, x]) + by_x(weight.at[0, yp, near_pair, x])
    arrived(z1[0])
    y1 = small_y(single(1))
    arrived(*x0)
    x0_on = small_x_on(single(0))
    slices += by_y(weight.at[0, y, other_pair, xn]) + by_y(weight.at[0, y, other_pair, xp])
    arrived(*z1[1:])
    x1 = small_x(single(1))
    arrived(*y0_on)
    slices += by_x(weight.at[0, yf, near_pair, x])
    arrived(*a2)
    a2_on = mail.same(weight.at[last, yn, z, :, rows_a], y=yp)
    arrived(*b2)
    b2_on = mail.same(weight.at[last, :, z, xn, rows_b], x=xp)
    arrived(*x0_on)
    slices += by_y(weight.at[0, y, other_pair, xf])
    big, big_done, plane = {}, {}, {}
    arrived(*y1)
    y1_on = small_y_on(single(1))
    arrived(*x1)
    x1_on = small_x_on(single(1))
    arrived(z2[0])
    y2 = small_y(double)
    arrived(*z2[1:])
    x2 = small_x(double)
    arrived(a2_on, b2_on)
    plane[0] = planes(0, 0), planes(0, 1)
    arrived(*y1_on)
    big[1] = big_x(1)
    arrived(*x1_on)
    big[1] += big_y(1)
    arrived(*y2)
    y2_on = small_y_on(double)
    arrived(*x2)
    x2_on = small_x_on(double)
    arrived(*slices)
    big_done[0] = big_on(0)
    planes_in(plane[0][0], 0)
    plane[1] = [planes(1, 0)]
    arrived(*y2_on, *x2_on)
    big[2] = big_x(2) + big_y(2)
    arrived(*big[1])
    big_done[1] = big_on(1)
    big[3] = big_x(3) + big_y(3)
    planes_in(plane[0][1], 0)
    plane[1] += [planes(1, 1)]
    arrived(*big_done[0])
    planes_in(plane[1][0], 1)
    plane[2] = [planes(2, 0)]
    attention(0)
    gather_back(0)
    arrived(*big[2])
    big_done[2] = big_on(2)
    arrived(*big_done[1])
    planes_in(plane[1][1], 1)
    plane[2] += [planes(2, 1)]
    attention(1)
    gather_back(1)
    arrived(*big[3])
    big_done[3] = big_on(3)
    arrived(*big_done[2])
    attention(2)
    gather_back(2)
    planes_in(plane[2][0], 2)
    planes_in(plane[2][1], 2)
    attention(4)
    gather_back(4)
    arrived(*big_done[3])
    attention(3)

    key_in = [mail.send(kv.at[0, to], kv_1.at[0, n], x=to) for n, to in enumerate((xp, xn, xf))]
    value_in = [mail.send(kv.at[1, :, to], kv_1.at[1, n], y=to) for n, to in enumerate((yp, yn, yf))]

    order = (0, 2, 1, 3)
    pair_in, far_in, up_in, down_in = {}, {}, {}, {}

    def make_part(j):
        whole = (made[j] + back(3, j)).astype(BF16)
        for t in range(8):
            part[j, t % 2, t // 2] = whole[t * 16 : (t + 1) * 16]
        pair_in[j] = mail.send(part.at[j, 1 - c], part_in.at[j], c=1 - c)

    def make_total(j):
        arrived(pair_in[j])
        total[j] = (part[j, c].astype(F32) + part_in[j].astype(F32)).astype(BF16)
        to = hp if j < 2 else hn
        far_in[j] = mail.send(total.at[j, hf], far.at[j], zh=to)

    def send_on(j):
        arrived(far_in[j])
        to = hp if j < 2 else hn
        relay[j] = (total[j, to].astype(F32) + far[j].astype(F32)).astype(BF16)
        if j < 2:
            up_in[j] = mail.send(relay.at[j], near_up.at[j], zh=hp)
        else:
            down_in[j] = mail.send(relay.at[j], near_down.at[j], zh=hn)

    make_part(0)
    make_part(2)
    make_part(1)
    make_total(0)
    make_part(3)
    make_total(2)
    make_total(1)
    make_total(3)
    for j in (0, 1):
        down_in[j] = mail.send(total.at[j, hn], near_down.at[j], zh=hn)
        up_in[j + 2] = mail.send(total.at[j + 2, hp], near_up.at[j + 2], zh=hp)

    arrived(*key_in)
    kv_mid[0] = kv[0, x] + kv_1[0, 0] + kv_1[0, 1] + kv_1[0, 2]
    key_in = [mail.send(kv_mid.at[0, to], kv_2.at[0, n], y=to) for n, to in enumerate((yp, yn, yf))]
    arrived(*value_in)
    kv_mid[1] = kv[1, :, y] + kv_1[1, 0] + kv_1[1, 1] + kv_1[1, 2]
    value_in = [mail.send(kv_mid.at[1, to], kv_2.at[1, n], x=to) for n, to in enumerate((xp, xn, xf))]
    send_on(0)
    send_on(2)
    arrived(*key_in, *value_in)
    for k, at in enumerate((y, x)):
        rows = kv_mid[k, at] + kv_2[k, 0] + kv_2[k, 1] + kv_2[k, 2]
        for j in range(4):
            kv_z_src[j, k] = rows[2 * j : 2 * j + 2]
    kv_z_in = [mail.send(kv_z_src.at[to], kv_z.at[n], zl=to) for n, to in enumerate(z_others)]
    send_on(1)
    send_on(3)

    for j in order:
        arrived(up_in[j], down_in[j])
        out_video[:, j * CHUNK : (j + 1) * CHUNK] = (
            total[j, h].astype(F32) + near_up[j].astype(F32) + near_down[j].astype(F32)
        ).astype(BF16)
    arrived(*kv_z_in)
    both = kv_z_src[z] + kv_z[0] + kv_z[1] + kv_z[2]
    out_keys[...] = both[0].astype(BF16)
    out_values[...] = both[1].astype(BF16)
    assert len(mail.made) == COPIES, len(mail.made)
    for copy in mail.sent:
        copy.wait_send()
    for copy, go in sent_if:
        pl.when(go)(copy.wait_send)


def hand_over(a_in, b_in, c_in, a_out, b_out, c_out):
    a_out[...] = a_in[...]
    b_out[...] = b_in[...]
    c_out[...] = c_in[...]


def local(video_tokens, w_query, text_keys, text_values, grad_out):
    vmem = pltpu.VMEM
    out_shape = (
        jax.ShapeDtypeStruct((16, DEPTH), BF16),
        jax.ShapeDtypeStruct((2, WIDTH), BF16),
        jax.ShapeDtypeStruct((2, WIDTH), BF16),
    )
    results = pl.pallas_call(
        kernel,
        out_shape=out_shape,
        in_specs=[pl.BlockSpec(memory_space=pl.ANY)] * 5,
        out_specs=(pl.BlockSpec(memory_space=pltpu.VMEM),) * 3,
        scratch_shapes=[
            vmem((TOKENS, DEPTH), BF16),
            vmem((TEXT, WIDTH), BF16),
            vmem((TEXT, WIDTH), BF16),
            vmem((TOKENS, WIDTH), BF16),
            vmem((TEXT, WIDTH), BF16),
            vmem((HEADS, 4, 4, 4, ROWS, HEAD_DIM), BF16),
            vmem((HEADS, TEXT, TOKENS), F32),
            vmem((TOKENS, WIDTH), BF16),
            vmem((4, TOKENS, CHUNK), F32),
            vmem((2, 4, 4, 8, WIDTH), F32),
            vmem((2, 3, 4, 8, WIDTH), F32),
            vmem((2, 3, 8, WIDTH), F32),
            vmem((2, 4, 8, WIDTH), F32),
            vmem((4, 2, 2, WIDTH), F32),
            vmem((3, 2, 2, WIDTH), F32),
            vmem((4, 2, 4, 16, CHUNK), BF16),
            vmem((4, 4, 16, CHUNK), BF16),
            vmem((4, 4, 16, CHUNK), BF16),
            vmem((4, 16, CHUNK), BF16),
            vmem((4, 16, CHUNK), BF16),
            vmem((4, 16, CHUNK), BF16),
            vmem((4, 16, CHUNK), BF16),
            pltpu.SemaphoreType.DMA((HEADS + 4,)),
            pltpu.SemaphoreType.DMA((COPIES,)),
            pltpu.SemaphoreType.DMA((COPIES,)),
        ],
        compiler_params=pltpu.CompilerParams(collective_id=0, has_side_effects=True),
    )(video_tokens, w_query, text_keys, text_values, grad_out)
    return pl.pallas_call(
        hand_over,
        out_shape=out_shape,
        in_specs=[pl.BlockSpec(memory_space=pltpu.VMEM)] * 3,
        out_specs=(pl.BlockSpec(memory_space=pltpu.VMEM),) * 3,
    )(*results)


def solution(mesh):
    split = Mesh(mesh.devices.reshape(4, 4, 4, 4, 2), AXES)
    tp = ("zh", "c")
    in_specs = (P(SEQ, None), P(SEQ, tp), P(None, tp), P(None, tp), P(SEQ, tp))
    out_specs = (P(AXES, None), P(SEQ, tp), P(SEQ, tp))
    return jax.shard_map(local, mesh=split, in_specs=in_specs, out_specs=out_specs, check_vma=False)
```

```python
import jax
import jax.numpy as jnp
from jax import lax
from jax.experimental import pallas as pl
from jax.experimental.pallas import tpu as pltpu
from jax.sharding import Mesh
from jax.sharding import PartitionSpec as P

HEAD_DIM = 128
HEADS = 5
ROWS = 80
TOKENS = 128
TEXT = 128
DEPTH = 5120
CHUNK = 1280
WIDTH = HEADS * HEAD_DIM
AXES = ("y", "zl", "x", "zh", "c")
SEQ = ("y", "zl", "x")
COPIES = 132
F32 = jnp.float32
BF16 = jnp.bfloat16


def dot(a, b, dims):
    return lax.dot_general(a, b, ((dims[:1], dims[1:]), ((), ())), preferred_element_type=F32)


class Mail:
    def __init__(self, send_sems, recv_sems):
        self.send_sems, self.recv_sems = send_sems, recv_sems
        self.made, self.sent = [], []

    def make(self, src, dst, **where):
        at = len(self.made)
        copy = pltpu.make_async_remote_copy(
            src_ref=src,
            dst_ref=dst,
            send_sem=self.send_sems.at[at],
            recv_sem=self.recv_sems.at[at],
            device_id=where,
            device_id_type=pl.DeviceIdType.MESH,
        )
        self.made.append(copy)
        return copy

    def send(self, src, dst, **where):
        copy = self.make(src, dst, **where)
        copy.start()
        self.sent.append(copy)
        return copy

    def same(self, ref, **where):
        return self.send(ref, ref, **where)


def arrived(*copies):
    for copy in copies:
        copy.wait_recv()


def kernel(
    video_hbm, weight_hbm, keys_hbm, values_hbm, grad_hbm,
    out_video, out_keys, out_values,
    video, keys_in, values_in, grad, keys, weight, grad_att, grad_query, made,
    kv, kv_1, kv_2, kv_mid, kv_z_src, kv_z,
    part, part_in, total, far, relay, near_up, near_down,
    local_sems, send_sems, recv_sems,
):
    y, z, x = lax.axis_index("y"), lax.axis_index("zl"), lax.axis_index("x")
    h, c = lax.axis_index("zh"), lax.axis_index("c")
    yf, xf = (y + 2) % 4, (x + 2) % 4
    yn, yp, xn, xp = (y + 3) % 4, (y + 1) % 4, (x + 3) % 4, (x + 1) % 4
    hn, hp, hf = (h + 3) % 4, (h + 1) % 4, (h + 2) % 4
    z_others = (z + 1 - 2 * (z % 2), (z + 2) % 4, 3 - z)
    near = 2 * (z // 2)
    other = 2 - near
    factor = HEAD_DIM ** (-0.5)

    own = [
        pltpu.make_async_copy(
            weight_hbm.at[:, pl.ds(k * HEAD_DIM, HEAD_DIM)], weight.at[k, y, z, x], local_sems.at[k]
        )
        for k in range(HEADS)
    ]
    loads = [
        pltpu.make_async_copy(src, dst, local_sems.at[HEADS + k])
        for k, (src, dst) in enumerate(
            ((keys_hbm, keys_in), (values_hbm, values_in), (grad_hbm, grad), (video_hbm, video))
        )
    ]
    for copy in own + loads:
        copy.start()

    barrier = pltpu.get_barrier_semaphore()
    partners = (
        [{"zl": k} for k in z_others]
        + [{"x": k} for k in (xp, xn, (x + 2) % 4)]
        + [{"y": k} for k in (yp, yn, (y + 2) % 4)]
        + [{"zh": hp}, {"zh": hn}, {"c": 1 - c}]
    )
    for where in partners:
        pl.semaphore_signal(barrier, inc=1, device_id=where, device_id_type=pl.DeviceIdType.MESH)
    pl.semaphore_wait(barrier, len(partners))
    for copy in own:
        copy.wait()

    mail = Mail(send_sems, recv_sems)
    near_pair, other_pair = pl.ds(near, 2), pl.ds(other, 2)

    def z_step(g):
        return [mail.same(weight.at[g, y, z, x], zl=k) for k in z_others]

    def small_y(g):
        ref = weight.at[g, y, near_pair, x]
        return mail.same(ref, y=yp), mail.same(ref, y=yn)

    def small_x(g):
        ref = weight.at[g, y, other_pair, x]
        return mail.same(ref, x=xp), mail.same(ref, x=xn)

    def small_y_on(g):
        return (
            mail.same(weight.at[g, yn, near, x], y=yp),
            mail.same(weight.at[g, yp, near + 1, x], y=yn),
        )

    def small_x_on(g):
        return (
            mail.same(weight.at[g, y, other, xn], x=xp),
            mail.same(weight.at[g, y, other + 1, xp], x=xn),
        )

    def big_x(k):
        ref = weight.at[k, :, near_pair, x]
        return mail.same(ref, x=xp), mail.same(ref, x=xn)

    def big_y(k):
        ref = weight.at[k, y, other_pair]
        return mail.same(ref, y=yp), mail.same(ref, y=yn)

    def big_on(k):
        return (
            mail.same(weight.at[k, :, near, xn], x=xp),
            mail.same(weight.at[k, :, near + 1, xp], x=xn),
            mail.same(weight.at[k, yn, other], y=yp),
            mail.same(weight.at[k, yp, other + 1], y=yn),
        )

    last = HEADS - 1
    rows_a, rows_b = pl.ds(0, 40), pl.ds(40, 40)
    single, double = (lambda k: pl.ds(k, 1)), pl.ds(2, 2)
    z0 = z_step(single(0))
    a_ref, b_ref = weight.at[last, y, z, x, rows_a], weight.at[last, y, z, x, rows_b]
    a1 = [mail.same(a_ref, x=to) for to in (xp, xn, (x + 2) % 4)]
    b1 = [mail.same(b_ref, y=to) for to in (yp, yn, (y + 2) % 4)]
    z1 = z_step(single(1))
    z2 = z_step(double)

    def by_x(ref):
        return mail.same(ref, x=xp), mail.same(ref, x=xn)

    def by_y(ref):
        return mail.same(ref, y=yp), mail.same(ref, y=yn)

    def columns(k):
        return slice(k * HEAD_DIM, (k + 1) * HEAD_DIM)

    for copy in loads[:3]:
        copy.wait()
    row = lax.broadcasted_iota(jnp.int32, (TEXT, TEXT), 0)
    col = lax.broadcasted_iota(jnp.int32, (TEXT, TEXT), 1)
    source = (row // 8 % 4) * 32 + (row // 2 % 4) * 8 + (row // 32) * 2 + row % 2
    pick = jnp.where(col == source, 1.0, 0.0).astype(BF16)
    keys[...] = dot(pick, keys_in[...], (1, 0)).astype(BF16)
    loads[3].wait()

    def prepare():
        for k in range(HEADS):
            values_k = dot(pick, values_in[:, columns(k)], (1, 0)).astype(BF16)
            grad_att[k] = dot(values_k, grad[:, columns(k)], (1, 1))

    def attention(k):
        parts = [
            dot(video[:, j * CHUNK : (j + 1) * CHUNK], weight[k, j].reshape(CHUNK, HEAD_DIM), (1, 0))
            for j in range(4)
        ]
        query = (parts[0] + parts[1] + (parts[2] + parts[3])).astype(BF16)
        keys_k = keys[:, columns(k)]
        scores = dot(keys_k, query, (1, 1)) * factor
        raised = jnp.exp(scores - jnp.max(scores, axis=0, keepdims=True))
        attend = raised / jnp.sum(raised, axis=0, keepdims=True)
        grad_attend = grad_att[k]
        row_dot = jnp.sum(attend * grad_attend, axis=0, keepdims=True)
        grad_scores = (attend * (grad_attend - row_dot) * factor).astype(BF16)
        grad_query[:, columns(k)] = dot(grad_scores, keys_k, (0, 0)).astype(BF16)
        key_part = dot(grad_scores, query, (1, 0))
        value_part = dot(attend.astype(BF16), grad[:, columns(k)], (1, 0))
        kv[0, :, :, :, columns(k)] = key_part.reshape(4, 4, 8, HEAD_DIM)
        kv[1, :, :, :, columns(k)] = value_part.reshape(4, 4, 8, HEAD_DIM)

    def back(k, j):
        return dot(grad_query[:, columns(k)], weight[k, j].reshape(CHUNK, HEAD_DIM), (1, 1))

    def gather_back(k):
        for j in range(4):
            made[j] = back(k, j) if k == 0 else made[j] + back(k, j)

    def small_a():
        ref = weight.at[last, y, z, :, rows_a]
        return mail.same(ref, y=yp), mail.same(ref, y=yn)

    def small_b():
        ref = weight.at[last, :, z, x, rows_b]
        return mail.same(ref, x=xp), mail.same(ref, x=xn)

    sent_if = []

    def plane_send(which, half, go, to):
        ref = weight.at[last, pl.ds(2 * half, 2), which]
        copy = mail.make(ref, ref, zl=to)
        pl.when(go)(copy.start)
        sent_if.append((copy, go))
        return copy

    def plane_arrived(copy, go):
        pl.when(go)(copy.wait_recv)

    z_up, z_down = (z + 1) % 4, (z + 3) % 4

    def planes(step, half):
        lower, upper = (z + 4 - step) % 4, (z + step) % 4
        up = plane_send(lower, half, jnp.logical_and(z >= step, z < 3), z_up)
        down = plane_send(upper, half, jnp.logical_and(z + step <= 3, z > 0), z_down)
        return up, down

    def planes_in(copies, step):
        plane_arrived(copies[0], z >= step + 1)
        plane_arrived(copies[1], z + step + 1 <= 3)

    prepare()
    arrived(*a1)
    a2 = small_a()
    arrived(*b1)
    b2 = small_b()
    arrived(z0[0])
    y0 = small_y(single(0))
    slices = by_x(weight.at[0, y, near_pair, x])
    arrived(*z0[1:])
    x0 = small_x(single(0))
    slices += by_y(weight.at[0, y, other_pair, x])
    arrived(*y0)
    y0_on = small_y_on(single(0))
    slices += by_x(weight.at[0, yn, near_pair, x]) + by_x(weight.at[0, yp, near_pair, x])
    arrived(z1[0])
    y1 = small_y(single(1))
    arrived(*x0)
    x0_on = small_x_on(single(0))
    slices += by_y(weight.at[0, y, other_pair, xn]) + by_y(weight.at[0, y, other_pair, xp])
    arrived(*z1[1:])
    x1 = small_x(single(1))
    arrived(*y0_on)
    slices += by_x(weight.at[0, yf, near_pair, x])
    arrived(*a2)
    a2_on = mail.same(weight.at[last, yn, z, :, rows_a], y=yp)
    arrived(*b2)
    b2_on = mail.same(weight.at[last, :, z, xn, rows_b], x=xp)
    arrived(*x0_on)
    slices += by_y(weight.at[0, y, other_pair, xf])
    big, big_done, plane = {}, {}, {}
    arrived(*y1)
    y1_on = small_y_on(single(1))
    arrived(*x1)
    x1_on = small_x_on(single(1))
    arrived(z2[0])
    y2 = small_y(double)
    arrived(*z2[1:])
    x2 = small_x(double)
    arrived(a2_on, b2_on)
    plane[0] = planes(0, 0), planes(0, 1)
    arrived(*y1_on)
    big[1] = big_x(1)
    arrived(*x1_on)
    big[1] += big_y(1)
    arrived(*y2)
    y2_on = small_y_on(double)
    arrived(*x2)
    x2_on = small_x_on(double)
    arrived(*slices)
    big_done[0] = big_on(0)
    planes_in(plane[0][0], 0)
    plane[1] = [planes(1, 0)]
    arrived(*y2_on, *x2_on)
    big[2] = big_x(2) + big_y(2)
    arrived(*big[1])
    big_done[1] = big_on(1)
    big[3] = big_x(3) + big_y(3)
    planes_in(plane[0][1], 0)
    plane[1] += [planes(1, 1)]
    arrived(*big_done[0])
    planes_in(plane[1][0], 1)
    plane[2] = [planes(2, 0)]
    attention(0)
    gather_back(0)
    arrived(*big[2])
    big_done[2] = big_on(2)
    arrived(*big_done[1])
    planes_in(plane[1][1], 1)
    plane[2] += [planes(2, 1)]
    attention(1)
    gather_back(1)
    arrived(*big[3])
    big_done[3] = big_on(3)
    arrived(*big_done[2])
    attention(2)
    gather_back(2)
    planes_in(plane[2][0], 2)
    planes_in(plane[2][1], 2)
    attention(4)
    gather_back(4)
    arrived(*big_done[3])
    attention(3)

    key_in = [mail.send(kv.at[0, to], kv_1.at[0, n], x=to) for n, to in enumerate((xp, xn, xf))]
    value_in = [mail.send(kv.at[1, :, to], kv_1.at[1, n], y=to) for n, to in enumerate((yp, yn, yf))]

    gathered = len(mail.sent)
    order = (0, 2, 1, 3)
    pair_in, far_in, up_in, down_in = {}, {}, {}, {}

    def make_part(j):
        whole = (made[j] + back(3, j)).astype(BF16)
        for t in range(8):
            part[j, t % 2, t // 2] = whole[t * 16 : (t + 1) * 16]
        pair_in[j] = mail.send(part.at[j, 1 - c], part_in.at[j], c=1 - c)

    def make_total(j):
        arrived(pair_in[j])
        total[j] = (part[j, c].astype(F32) + part_in[j].astype(F32)).astype(BF16)
        to = hp if j < 2 else hn
        far_in[j] = mail.send(total.at[j, hf], far.at[j], zh=to)

    def send_on(j):
        arrived(far_in[j])
        to = hp if j < 2 else hn
        relay[j] = (total[j, to].astype(F32) + far[j].astype(F32)).astype(BF16)
        if j < 2:
            up_in[j] = mail.send(relay.at[j], near_up.at[j], zh=hp)
        else:
            down_in[j] = mail.send(relay.at[j], near_down.at[j], zh=hn)

    make_part(0)
    make_part(2)
    make_part(1)
    make_total(0)
    make_part(3)
    make_total(2)
    make_total(1)
    make_total(3)
    for j in (0, 1):
        down_in[j] = mail.send(total.at[j, hn], near_down.at[j], zh=hn)
        up_in[j + 2] = mail.send(total.at[j + 2, hp], near_up.at[j + 2], zh=hp)

    arrived(*key_in)
    kv_mid[0] = kv[0, x] + kv_1[0, 0] + kv_1[0, 1] + kv_1[0, 2]
    key_in = [mail.send(kv_mid.at[0, to], kv_2.at[0, n], y=to) for n, to in enumerate((yp, yn, yf))]
    arrived(*value_in)
    kv_mid[1] = kv[1, :, y] + kv_1[1, 0] + kv_1[1, 1] + kv_1[1, 2]
    value_in = [mail.send(kv_mid.at[1, to], kv_2.at[1, n], x=to) for n, to in enumerate((xp, xn, xf))]
    send_on(0)
    send_on(2)
    arrived(*key_in, *value_in)
    for k, at in enumerate((y, x)):
        rows = kv_mid[k, at] + kv_2[k, 0] + kv_2[k, 1] + kv_2[k, 2]
        for j in range(4):
            kv_z_src[j, k] = rows[2 * j : 2 * j + 2]
    kv_z_in = [mail.send(kv_z_src.at[to], kv_z.at[n], zl=to) for n, to in enumerate(z_others)]
    send_on(1)
    send_on(3)

    for copy in mail.sent[:gathered]:
        copy.wait_send()
    for copy, go in sent_if:
        pl.when(go)(copy.wait_send)
    for j in order:
        arrived(up_in[j], down_in[j])
        out_video[:, j * CHUNK : (j + 1) * CHUNK] = (
            total[j, h].astype(F32) + near_up[j].astype(F32) + near_down[j].astype(F32)
        ).astype(BF16)
    arrived(*kv_z_in)
    both = kv_z_src[z] + kv_z[0] + kv_z[1] + kv_z[2]
    out_keys[...] = both[0].astype(BF16)
    out_values[...] = both[1].astype(BF16)
    assert len(mail.made) == COPIES, len(mail.made)
    for copy in mail.sent[gathered:]:
        copy.wait_send()


def hand_over(a_in, b_in, c_in, a_out, b_out, c_out):
    a_out[...] = a_in[...]
    b_out[...] = b_in[...]
    c_out[...] = c_in[...]


def local(video_tokens, w_query, text_keys, text_values, grad_out):
    vmem = pltpu.VMEM
    out_shape = (
        jax.ShapeDtypeStruct((16, DEPTH), BF16),
        jax.ShapeDtypeStruct((2, WIDTH), BF16),
        jax.ShapeDtypeStruct((2, WIDTH), BF16),
    )
    results = pl.pallas_call(
        kernel,
        out_shape=out_shape,
        in_specs=[pl.BlockSpec(memory_space=pl.ANY)] * 5,
        out_specs=(pl.BlockSpec(memory_space=pltpu.VMEM),) * 3,
        scratch_shapes=[
            vmem((TOKENS, DEPTH), BF16),
            vmem((TEXT, WIDTH), BF16),
            vmem((TEXT, WIDTH), BF16),
            vmem((TOKENS, WIDTH), BF16),
            vmem((TEXT, WIDTH), BF16),
            vmem((HEADS, 4, 4, 4, ROWS, HEAD_DIM), BF16),
            vmem((HEADS, TEXT, TOKENS), F32),
            vmem((TOKENS, WIDTH), BF16),
            vmem((4, TOKENS, CHUNK), F32),
            vmem((2, 4, 4, 8, WIDTH), F32),
            vmem((2, 3, 4, 8, WIDTH), F32),
            vmem((2, 3, 8, WIDTH), F32),
            vmem((2, 4, 8, WIDTH), F32),
            vmem((4, 2, 2, WIDTH), F32),
            vmem((3, 2, 2, WIDTH), F32),
            vmem((4, 2, 4, 16, CHUNK), BF16),
            vmem((4, 4, 16, CHUNK), BF16),
            vmem((4, 4, 16, CHUNK), BF16),
            vmem((4, 16, CHUNK), BF16),
            vmem((4, 16, CHUNK), BF16),
            vmem((4, 16, CHUNK), BF16),
            vmem((4, 16, CHUNK), BF16),
            pltpu.SemaphoreType.DMA((HEADS + 4,)),
            pltpu.SemaphoreType.DMA((COPIES,)),
            pltpu.SemaphoreType.DMA((COPIES,)),
        ],
        compiler_params=pltpu.CompilerParams(collective_id=0, has_side_effects=True),
    )(video_tokens, w_query, text_keys, text_values, grad_out)
    return pl.pallas_call(
        hand_over,
        out_shape=out_shape,
        in_specs=[pl.BlockSpec(memory_space=pltpu.VMEM)] * 3,
        out_specs=(pl.BlockSpec(memory_space=pltpu.VMEM),) * 3,
    )(*results)


def solution(mesh):
    split = Mesh(mesh.devices.reshape(4, 4, 4, 4, 2), AXES)
    tp = ("zh", "c")
    in_specs = (P(SEQ, None), P(SEQ, tp), P(None, tp), P(None, tp), P(SEQ, tp))
    out_specs = (P(AXES, None), P(SEQ, tp), P(SEQ, tp))
    return jax.shard_map(local, mesh=split, in_specs=in_specs, out_specs=out_specs, check_vma=False)
```
